32 devices in a mesh: parts: 2 (over x), dp: 4 (over y, core), feat: 4 (over z).
Axes of the slice: x: 2, y: 2, z: 4, core: 2. Of those that a mesh axis runs over, the one named last changes fastest.
Arguments:
- train_grads: bfloat16 [8192, 8192], P(('parts', 'dp'), 'feat'), parts along dimension 0, may hold values from -6 to 6
- eval_grads: bfloat16 [1024, 8192], P(('parts', 'feat'), 'dp'), parts along dimension 0, may hold values from -6 to 6
- kinv: bfloat16 [8192, 8192], P('feat', 'dp'), may hold values from -0.5 to 2
Outputs:
- scores: bfloat16 [1024, 4096], P(('parts', 'feat'), 'dp'), parts along dimension 0
The draws below stay inside these ranges and needn't reach their ends.
There are 2 independent parts, one for each index of `parts`. The reference program is written for one: setup_inputs(seed, part) draws one part's arguments, and reference() takes and returns one part's arrays. A program takes and returns all parts, laid end to end along the dimension named above; an argument that names none is the same for every part. Nothing has to cross between parts.
All inputs are finite; a program needn't handle non-finite values.
Results may differ from the reference program's by a relative error of at most 0.0049.
Values may be sent and summed in bfloat16 or wider, within the bound.
No kernel may reach another device: no remote copies, remote signals or barrier semaphores. Data moves between devices by JAX's collectives and lax.ppermute only.
A program may use at most 64 MiB of HBM per device.

```python
import math
import jax
import jax.numpy as jnp
from jax import lax

P_SIZE = 8192
NTR = 4096
NEV = 512


def draw_kinv(key, part):
    row_index = lax.broadcasted_iota(jnp.int32, (P_SIZE, P_SIZE), 0)
    col_index = lax.broadcasted_iota(jnp.int32, (P_SIZE, P_SIZE), 1)
    noise = jnp.clip(jax.random.normal(key, (P_SIZE, P_SIZE), jnp.float32), -4.0, 4.0)
    values = jnp.where(row_index == col_index, 1.5, 0.0) + noise * (1.0 / math.sqrt(P_SIZE))
    return values.astype(jnp.bfloat16)


def spiked(array, rng, source, target, blocks, factor):
    owner, partner = [(jnp.arange(array.shape[position]) // (array.shape[position] // blocks)).reshape([-1 if axis == position else 1 for axis in range(array.ndim)]) for position in (source, target)]
    chosen = jax.random.permutation(rng, blocks)[partner]
    strong = (owner == chosen) | (owner == (partner + blocks // 2) % blocks)
    return jnp.where(strong, factor * array, array)


def level_of(rng, shape, cuts, low, largest):
    level, own = 1.0, jax.random.fold_in(rng, 6)
    for axis_at, blocks in cuts:
        heights = jnp.exp(jax.random.uniform(jax.random.fold_in(own, axis_at), (blocks,), jnp.float32, low / len(cuts), largest / len(cuts)))
        level = level * jnp.repeat(heights, shape[axis_at] // blocks).reshape([-1 if axis == axis_at else 1 for axis in range(len(shape))])
    return level


def bell_draw(stream_key, extent, deviation, most, split=(), kind=jnp.bfloat16):
    array = deviation * jax.random.normal(stream_key, extent, jnp.float32)
    if split:
        array = array * level_of(stream_key, extent, split, -0.22, 0.18)
    return jnp.clip(array, -most, most).astype(kind)


def noise_with(stream_key, dims, width, most, shards, heavy, kind=jnp.bfloat16):
    result = width * jax.random.normal(stream_key, dims, jnp.float32)
    if shards:
        result = result * level_of(stream_key, dims, shards, -0.22, 0.18)
    return jnp.clip(spiked(result, jax.random.fold_in(stream_key, 3), *heavy), -most, most).astype(kind)


def setup_inputs(seed: int = 0, part: int = 0) -> dict:
    streams_of = jax.random.split(jax.random.key(seed), 4)
    part_splits = jax.random.split(jax.random.fold_in(streams_of[3], part), 4)
    train_grads = bell_draw(part_splits[0], (NTR, P_SIZE), 1.0, 6.0, ((0, 4), (1, 4)))
    eval_grads = noise_with(part_splits[1], (NEV, P_SIZE), 1.0, 6.0, ((0, 4), (1, 4)), (1, 0, 4, 2.0))
    kinv = draw_kinv(jax.random.fold_in(streams_of[3], 71), part)
    return dict(train_grads=train_grads, eval_grads=eval_grads, kinv=kinv)


def contract(left, right):
    return lax.dot_general(left, right, (((1,), (1,)), ((), ())), preferred_element_type=jnp.float32)

def reference(train_grads, eval_grads, kinv):
    precond = contract(eval_grads, kinv).astype(jnp.bfloat16)
    summed = contract(precond, train_grads)
    return (summed * (1.0 / math.sqrt(P_SIZE))).astype(jnp.bfloat16)
```

```python
import functools
import math

import jax
import jax.numpy as jnp
from jax import lax
from jax.experimental import pallas as pl
from jax.experimental.pallas import tpu as pltpu
from jax.sharding import PartitionSpec as P

P_SIZE = 8192
SCALE = 1.0 / math.sqrt(P_SIZE)
BF16, F32 = jnp.bfloat16, jnp.float32
VMEM = pltpu.MemorySpace.VMEM
SMEM = pltpu.MemorySpace.SMEM


def contract(left, right):
    return lax.dot_general(
        left, right, (((1,), (1,)), ((), ())), preferred_element_type=F32
    )


def general(train_grads, eval_grads, kinv):
    evals_all = lax.all_gather(eval_grads, "feat", axis=0, tiled=True)
    precond = lax.psum(contract(evals_all, kinv), "dp").astype(BF16)
    summed = lax.psum_scatter(
        contract(precond, train_grads), "feat", scatter_dimension=0, tiled=True
    )
    return (summed * SCALE).astype(BF16)


def params(limit=24 << 20):
    return pltpu.CompilerParams(vmem_limit_bytes=limit)


def spec(space):
    return pl.BlockSpec(memory_space=space)


def joined(refs, how):
    values = [ref[...] for ref in refs]
    if how == "rows":
        return values[0] if len(values) == 1 else jnp.concatenate(values, axis=0)
    return functools.reduce(lambda a, b: a + b, values)


TILE = 512


def first_body(count, how, half_ref, *refs):
    evals, (kinv_ref, send_ref, keep_ref) = refs[:count], refs[count:]
    half = half_ref[0]
    left = joined(evals, how)
    size = send_ref.shape[1]
    for out_ref, which in ((send_ref, 1 - half), (keep_ref, half)):
        for start in range(0, size, TILE):
            rows = pl.ds(pl.multiple_of(which * size + start, TILE), TILE)
            out_ref[:, start : start + TILE] = contract(left, kinv_ref[rows, :]).astype(
                out_ref.dtype
            )


def first(half, evals, kinv, how="rows"):
    rows = evals[0].shape[0] * (len(evals) if how == "rows" else 1)
    size = kinv.shape[0] // 2
    return pl.pallas_call(
        functools.partial(first_body, len(evals), how),
        in_specs=[spec(SMEM)] + [spec(VMEM)] * (len(evals) + 1),
        out_specs=[spec(VMEM)] * 2,
        out_shape=[
            jax.ShapeDtypeStruct((rows, size), BF16),
            jax.ShapeDtypeStruct((rows, size), F32),
        ],
        compiler_params=params(),
        cost_estimate=pl.CostEstimate(
            flops=4 * 256 * kinv.shape[0] * kinv.shape[1],
            bytes_accessed=rows * size * 6,
            transcendentals=0,
        ),
        name="first",
    )(half, *evals, kinv)


def second_body(half_ref, own_ref, other_ref, train_ref, out_ref):
    half = half_ref[0]
    size = own_ref.shape[1]
    for start in range(0, out_ref.shape[1], TILE):
        total = None
        for ref, which in ((own_ref, half), (other_ref, 1 - half)):
            columns = pl.ds(pl.multiple_of(which * size, size), size)
            term = contract(ref[...], train_ref[start : start + TILE, columns])
            total = term if total is None else total + term
        out_ref[:, start : start + TILE] = total.astype(out_ref.dtype)


def second(half, own, other, train, dtype):
    rows = own.shape[0]
    return pl.pallas_call(
        second_body,
        in_specs=[spec(SMEM)] + [spec(VMEM)] * 3,
        out_specs=spec(VMEM),
        out_shape=jax.ShapeDtypeStruct((rows, train.shape[0]), dtype),
        compiler_params=params(),
        cost_estimate=pl.CostEstimate(
            flops=4 * 256 * train.shape[0] * train.shape[1],
            bytes_accessed=rows * train.shape[0] * 4,
            transcendentals=0,
        ),
        name="second",
    )(half, own, other, train)


def line_of_four(train, evals, kinv):
    half = (lax.axis_index("dp") % 2).astype(jnp.int32).reshape(1)

    def over_feat(x, pairs):
        return lax.ppermute(x, "feat", pairs)

    def over_core(x):
        return lax.ppermute(x, "dp", [(i, i ^ 1) for i in range(4)])

    def over_y(x):
        return lax.ppermute(x, "dp", [(i, i ^ 2) for i in range(4)])

    def xor(k):
        return [(i, i ^ k) for i in range(4)]

    def chain(blocks, how, dtype):
        send, keep = first(half, blocks, kinv, how)
        keep = keep + over_core(send).astype(F32)
        whole = (keep + over_y(keep.astype(BF16)).astype(F32)).astype(BF16)
        return second(half, whole, over_core(whole), train, dtype)

    near = over_feat(evals, xor(1))
    middle = over_feat(evals, [(1, 2), (2, 1)])
    next_middle = over_feat(near, [(1, 2), (2, 1)])
    next_end = over_feat(middle, [(1, 0), (2, 3)])
    last_end = over_feat(next_middle, [(1, 0), (2, 3)])
    size = evals.shape[0]

    own = chain([evals], "rows", F32)
    pair = chain([near, middle], "rows", BF16)
    from_near = over_feat(pair[:size], xor(1))
    from_middle = over_feat(pair[size:], [(1, 2), (2, 1)])
    far = chain([next_middle, next_end], "sum", BF16)
    from_far = over_feat(far, xor(2))
    end = chain([last_end], "rows", BF16)
    from_end = over_feat(end, [(0, 3), (3, 0)])
    total = own
    for part in (from_near, from_middle, from_far, from_end):
        total = total + part.astype(F32)
    return (total * SCALE).astype(BF16)


def solution(mesh):
    in_specs = (P(("parts", "dp"), "feat"), P(("parts", "feat"), "dp"), P("feat", "dp"))
    out_specs = P(("parts", "feat"), "dp")
    four = mesh.shape["dp"] == 4 and mesh.shape["feat"] == 4
    return jax.shard_map(
        line_of_four if four else general,
        mesh=mesh,
        in_specs=in_specs,
        out_specs=out_specs,
        check_vma=False,
    )
```
